32 devices in a mesh: section: 4 (over y, x), dom: 8 (over z, core).
Axes of the slice: x: 2, y: 2, z: 4, core: 2. Of those that a mesh axis runs over, the one named last changes fastest.
Arguments:
- stacked: bfloat16 [4, 1024, 1024], P('section', 'dom'), may hold values from -6 to 6
- edges: int32 [1024, 256], P('dom'), may hold values 0 or 1
- picks: int32 [16, 3], P('dom'), may hold values from 0 to 2
- self_w: bfloat16 [4, 1024, 1024], P('section'), may hold values from -0.1875 to 0.1875
- neigh_w: bfloat16 [4, 1024, 1024], P('section'), may hold values from -0.75 to 0.75
Outputs:
- embeddings: bfloat16 [4, 1024, 1024], P('section', 'dom')
The draws below stay inside these ranges and needn't reach their ends.
Inputs may be any that keep to these rules, and one draw needn't show every extreme that they name: `picks`: A value of 2 means that the destination block has no tile from that direction; smaller values name a slab of the peer partition.
All inputs are finite; a program needn't handle non-finite values. No bound on the sum of `edges` on one device may be relied on, other than what follows from the above.
Results may differ from the reference program's by a relative error of at most 0.006.
Values may be sent and summed in bfloat16 or wider, within the bound.
A program may use at most 64 MiB of HBM per device.

```python
import jax
import jax.numpy as jnp

D = 1024
BLOCK = 64
SLABS = 2
LAYERS = 4
NODES = 1024
N_DOM = 8


def place_ends(entries, rng, low, high):
    longest = entries.shape.index(max(entries.shape))
    spots = []
    for shift in (0, 1):
        where = [jax.random.randint(jax.random.fold_in(rng, axis), (), 0, length) for axis, length in enumerate(entries.shape)]
        where[longest] = (where[longest] + shift) % entries.shape[longest]
        spots.append(tuple(where))
    return entries.at[spots[0]].set(low).at[spots[1]].set(high)


def levels(stream_key, extent, cuts, smallest, top_value):
    level = 1.0
    for dim, blocks in cuts:
        heights = jax.random.uniform(jax.random.fold_in(jax.random.fold_in(stream_key, 6), dim), (blocks,), jnp.float32, smallest / len(cuts), top_value / len(cuts))
        level = level * jnp.repeat(jnp.exp(heights), extent[dim] // blocks).reshape((-1,) + (1,) * (len(extent) - 1 - dim))
    return level


def gaussian(rng, shape, width, most, pieces=(), held_as=jnp.bfloat16):
    entries = jax.random.normal(rng, shape, jnp.float32) * width
    if len(pieces) > 0:
        entries = levels(rng, shape, pieces, -0.22, 0.18) * entries
    return jnp.clip(entries, min=-most, max=most).astype(held_as)


def setup_inputs(seed: int = 0) -> dict:
    arg_keys = jax.random.split(jax.random.key(seed), 6)
    stacked = gaussian(arg_keys[0], (LAYERS, NODES, D), 1.0, 6.0, ((0, 4), (1, 8)))
    edges = place_ends((jax.random.randint(arg_keys[1], (NODES, 4 * BLOCK), 0, 16) < 1).astype(jnp.int32), jax.random.fold_in(arg_keys[1], 1), 0, 1)
    picks = place_ends(jax.random.randint(arg_keys[2], (NODES // BLOCK, 3), 0, SLABS + 1), jax.random.fold_in(arg_keys[2], 1), 0, SLABS).astype(jnp.int32)
    self_w = gaussian(arg_keys[3], (LAYERS, D, D), D ** -0.5, 0.1875, ((0, 4),))
    neigh_w = gaussian(arg_keys[4], (LAYERS, D, D), (D // 16) ** -0.5, 0.75, ((0, 4),))
    return {"stacked": stacked, "edges": edges, "picks": picks, "self_w": self_w, "neigh_w": neigh_w}


def reference(stacked, edges, picks, self_w, neigh_w):
    layer_count = stacked.shape[0]
    node_total = stacked.shape[1]
    feature_width = stacked.shape[2]
    partitions = N_DOM
    peer_offsets = (-1, 1, 2)
    tile_table = edges.reshape(partitions, SLABS, BLOCK, 4, BLOCK)
    pick_table = picks.reshape(partitions, SLABS, 3)
    live_tiles = (pick_table < SLABS).astype(jnp.float32)
    clamped = jnp.minimum(pick_table, SLABS - 1).astype(jnp.int32)
    partition_ids = jnp.arange(partitions).astype(jnp.int32)
    current = stacked[0].reshape(partitions, SLABS, BLOCK, feature_width)
    results = []
    for layer_index in range(layer_count):
        history = stacked[layer_index].reshape(partitions, SLABS, BLOCK, feature_width)
        produced = []
        for slab_now in range(SLABS):
            fresh_mask = (jnp.arange(SLABS) <= slab_now)[None, :, None, None]
            source = jnp.where(fresh_mask, current, history)
            own_rows = current[:, slab_now]
            tile_zero = tile_table[:, slab_now, :, 0, :].astype(jnp.float32)
            summed = jnp.einsum("pij,pjd->pid", tile_zero, own_rows.astype(jnp.float32))
            degree = 1.0 + jnp.sum(tile_zero, axis=-1)
            for position in range(3):
                peer_field = jnp.roll(source, -peer_offsets[position], axis=0)
                blocks = peer_field[partition_ids, clamped[:, slab_now, position]]
                tile_mask = tile_table[:, slab_now, :, position + 1, :].astype(jnp.float32)
                tile_mask = tile_mask * live_tiles[:, slab_now, position][:, None, None]
                summed = summed + jnp.einsum("pij,pjd->pid", tile_mask, blocks.astype(jnp.float32))
                degree = degree + jnp.sum(tile_mask, axis=-1)
            mean_rows = (summed / degree[..., None]).astype(jnp.bfloat16)
            hidden = jnp.dot(own_rows.reshape(-1, feature_width), self_w[layer_index], preferred_element_type=jnp.float32)
            hidden = hidden + jnp.dot(mean_rows.reshape(-1, feature_width), neigh_w[layer_index], preferred_element_type=jnp.float32)
            produced.append(jnp.maximum(hidden, 0.0).astype(jnp.bfloat16).reshape(partitions, BLOCK, feature_width))
        current = jnp.stack(produced, axis=1)
        results.append(current.reshape(node_total, feature_width))
    return jnp.stack(results)
```

```python
import functools

import jax
import jax.numpy as jnp
from jax import lax
from jax.experimental import pallas as pl
from jax.experimental.pallas import tpu as pltpu
from jax.sharding import PartitionSpec as P

PEER_OFFSETS = (-1, 1, 2)
MESH = pl.DeviceIdType.MESH


def kernel(
    ns, nd, slabs, nch,
    stacked, edges, picks, ws_hbm, wn_hbm, out,
    ws, wn, src, masks, pre, acc, stage,
    wsem, zsend, zrecv, xsend, xrecv,
):
    block = edges.shape[1] // (len(PEER_OFFSETS) + 1)
    width = stacked.shape[1]
    cw = width // nch
    s = lax.axis_index("section")
    p = lax.axis_index("dom")

    def at(section, dom):
        return {"section": section, "dom": dom}

    w_self = pltpu.make_async_copy(ws_hbm, ws, wsem.at[0])
    w_neigh = pltpu.make_async_copy(wn_hbm, wn, wsem.at[1])
    w_self.start()
    w_neigh.start()

    barrier = pltpu.get_barrier_semaphore()
    greeted = [at(s, lax.rem(p + o + nd, nd)) for o in (-2, -1, 1, 2)]
    greeted += [at(lax.rem(s + 1, ns), p), at(lax.rem(s + ns - 1, ns), p)]
    for device in greeted:
        pl.semaphore_signal(barrier, inc=1, device_id=device, device_id_type=MESH)

    def rows(c):
        return pl.ds(c * block, block)

    def cols(ch):
        return pl.ds(ch * cw, cw)

    last = slabs - 1
    later = last * ((s + ns - 1) // ns)

    def fresh_slot(c):
        return c if c == 0 else c + later

    def z_copy(src_ref, slot, ch, k):
        return pltpu.make_async_remote_copy(
            src_ref=src_ref,
            dst_ref=src.at[slot, rows(k + 1), cols(ch)],
            send_sem=zsend.at[slot, ch, k],
            recv_sem=zrecv.at[slot, ch, k],
            device_id=at(s, lax.rem(p - PEER_OFFSETS[k] + nd, nd)),
            device_id_type=MESH,
        )

    def x_copy(c, ch):
        return pltpu.make_async_remote_copy(
            src_ref=stage.at[c, :, cols(ch)],
            dst_ref=src.at[0 if c == 0 else c + last, rows(0), cols(ch)],
            send_sem=xsend.at[c, ch],
            recv_sem=xrecv.at[c, ch],
            device_id=at(lax.rem(s + 1, ns), p),
            device_id_type=MESH,
        )

    def given(j, ch):
        return stacked.at[rows(j), cols(ch)]

    def own(slot, ch):
        return src.at[slot, rows(0), cols(ch)]

    tile = lax.broadcasted_iota(jnp.int32, (block, edges.shape[1]), 1) // block
    degree = []
    for c in range(slabs):
        entries = edges[rows(c), :].astype(jnp.float32)
        total = jnp.ones((block, 1), jnp.float32)
        for j in range(slabs):
            scale = jnp.full(entries.shape, 1.0 if c == j else 0.0, jnp.float32)
            for k in range(len(PEER_OFFSETS)):
                wanted = jnp.where(picks[c, k] == j, 1.0, 0.0)
                scale = jnp.where(tile == k + 1, wanted, scale)
            masked = entries * scale
            masks[c, j] = masked.astype(jnp.bfloat16)
            total = total + jnp.sum(masked, axis=1, keepdims=True)
        degree.append(total)
    for j in range(1, slabs):
        src[j, rows(0), :] = stacked[rows(j), :]

    @pl.when(s == 0)
    def _():
        src[0, rows(0), :] = stacked[rows(0), :]

    pl.semaphore_wait(barrier, len(greeted))

    for ch in range(nch):
        @pl.when(s == 0)
        def _():
            for k in range(len(PEER_OFFSETS)):
                z_copy(given(0, ch), 0, ch, k).start()
        for j in range(1, slabs):
            for k in range(len(PEER_OFFSETS)):
                z_copy(given(j, ch), j, ch, k).start()

    def gather(c, j, slot, ch):
        return jnp.dot(
            masks[c, j], src[slot, :, cols(ch)], preferred_element_type=jnp.float32
        )

    def z_wait(slot, ch):
        for k in range(len(PEER_OFFSETS)):
            z_copy(own(slot, ch), slot, ch, k).wait_recv()

    w_self.wait()

    for c in range(slabs):
        slot = fresh_slot(c)
        for ch in range(nch):
            @pl.when(s > 0)
            def _():
                x_copy(c, ch).wait_recv()
                for k in range(len(PEER_OFFSETS)):
                    z_copy(own(slot, ch), slot, ch, k).start()
        for ch in range(nch):
            part = jnp.dot(
                src[slot, rows(0), cols(ch)], ws[cols(ch), :],
                preferred_element_type=jnp.float32,
            )
            if ch == 0:
                acc[...] = part
            else:
                acc[...] += part
        if c == 0:
            w_neigh.wait()
        for ch in range(nch):
            if c == 0:
                for j in range(1, slabs):
                    z_wait(j, ch)
            part = None
            for j in range(slabs):
                if j != c:
                    term = gather(c, j, fresh_slot(j) if j < c else j, ch)
                    part = term if part is None else part + term
            pre[:, cols(ch)] = part
        for ch in range(nch):
            if c == 0:
                z_wait(slot, ch)
            else:
                @pl.when(s > 0)
                def _():
                    z_wait(slot, ch)
            summed = pre[:, cols(ch)] + gather(c, c, slot, ch)
            mean = (summed / degree[c]).astype(jnp.bfloat16)
            if ch < nch - 1:
                acc[...] += jnp.dot(mean, wn[cols(ch), :], preferred_element_type=jnp.float32)
            else:
                for n in range(nch):
                    hidden = acc[:, cols(n)] + jnp.dot(
                        mean, wn[cols(ch), cols(n)], preferred_element_type=jnp.float32
                    )
                    stage[c, :, cols(n)] = jnp.maximum(hidden, 0.0).astype(jnp.bfloat16)

                    @pl.when(s < ns - 1)
                    def _():
                        x_copy(c, n).start()
        out[rows(c), :] = stage[c]

    for ch in range(nch):
        for k in range(len(PEER_OFFSETS)):
            for slot in range(slabs):
                z_copy(own(slot, ch), slot, ch, k).wait_send()
            for c in range(1, slabs):
                @pl.when(s > 0)
                def _():
                    z_copy(own(c + last, ch), c + last, ch, k).wait_send()
        for c in range(slabs):
            @pl.when(s < ns - 1)
            def _():
                x_copy(c, ch).wait_send()


def per_device(ns, nd, stacked, edges, picks, self_w, neigh_w):
    _, node_rows, width = stacked.shape
    tiles = len(PEER_OFFSETS) + 1
    block = edges.shape[1] // tiles
    slabs = node_rows // block
    nch = max(1, width // 256)
    slots = 2 * slabs - 1
    vmem = pl.BlockSpec(memory_space=pltpu.VMEM)
    hbm = pl.BlockSpec(memory_space=pl.ANY)
    result = pl.pallas_call(
        functools.partial(kernel, ns, nd, slabs, nch),
        out_shape=jax.ShapeDtypeStruct((node_rows, width), jnp.bfloat16),
        in_specs=[vmem, vmem, pl.BlockSpec(memory_space=pltpu.SMEM), hbm, hbm],
        out_specs=vmem,
        scratch_shapes=[
            pltpu.VMEM((width, width), jnp.bfloat16),
            pltpu.VMEM((width, width), jnp.bfloat16),
            pltpu.VMEM((slots, tiles * block, width), jnp.bfloat16),
            pltpu.VMEM((slabs, slabs, block, tiles * block), jnp.bfloat16),
            pltpu.VMEM((block, width), jnp.float32),
            pltpu.VMEM((block, width), jnp.float32),
            pltpu.VMEM((slabs, block, width), jnp.bfloat16),
            pltpu.SemaphoreType.DMA((2,)),
            pltpu.SemaphoreType.DMA((slots, nch, tiles - 1)),
            pltpu.SemaphoreType.DMA((slots, nch, tiles - 1)),
            pltpu.SemaphoreType.DMA((slabs, nch)),
            pltpu.SemaphoreType.DMA((slabs, nch)),
        ],
        compiler_params=pltpu.CompilerParams(collective_id=0, has_side_effects=True),
    )(stacked[0], edges, picks, self_w[0], neigh_w[0])
    return result[None]


def solution(mesh):
    in_specs = (
        P("section", "dom", None),
        P("dom", None),
        P("dom", None),
        P("section", None, None),
        P("section", None, None),
    )
    out_specs = P("section", "dom", None)
    ns, nd = mesh.shape["section"], mesh.shape["dom"]
    return jax.shard_map(
        functools.partial(per_device, ns, nd),
        mesh=mesh, in_specs=in_specs, out_specs=out_specs, check_vma=False,
    )
```

```python
import functools

import jax
import jax.numpy as jnp
from jax import lax
from jax.experimental import pallas as pl
from jax.experimental.pallas import tpu as pltpu
from jax.sharding import PartitionSpec as P

PEER_OFFSETS = (-1, 1, 2)
MESH = pl.DeviceIdType.MESH


def kernel(
    ns, nd, slabs, nch,
    stacked, edges, picks, ws_hbm, wn_hbm, out,
    ws, wn, src, masks, pre, acc, stage,
    wsem, zsend, zrecv, xsend, xrecv,
):
    block = edges.shape[1] // (len(PEER_OFFSETS) + 1)
    width = stacked.shape[1]
    cw = width // nch
    s = lax.axis_index("section")
    p = lax.axis_index("dom")

    def at(section, dom):
        return {"section": section, "dom": dom}

    w_self = pltpu.make_async_copy(ws_hbm, ws, wsem.at[0])
    w_neigh = pltpu.make_async_copy(wn_hbm, wn, wsem.at[1])
    w_self.start()
    w_neigh.start()

    barrier = pltpu.get_barrier_semaphore()
    greeted = [at(s, lax.rem(p + o + nd, nd)) for o in (-2, -1, 1, 2)]
    greeted += [at(lax.rem(s + 1, ns), p), at(lax.rem(s + ns - 1, ns), p)]
    for device in greeted:
        pl.semaphore_signal(barrier, inc=1, device_id=device, device_id_type=MESH)

    def rows(c):
        return pl.ds(c * block, block)

    def cols(ch):
        return pl.ds(ch * cw, cw)

    last = slabs - 1
    later = last * ((s + ns - 1) // ns)

    def fresh_slot(c):
        return c if c == 0 else c + later

    even = lax.rem(p, 2) == 0
    partner = p + 1 - 2 * lax.rem(p, 2)
    far = len(PEER_OFFSETS) - 1

    def z_copy(src_ref, slot, ch, k):
        return pltpu.make_async_remote_copy(
            src_ref=src_ref,
            dst_ref=src.at[slot, rows(k + 1), cols(ch)],
            send_sem=zsend.at[slot, ch, k],
            recv_sem=zrecv.at[slot, ch, k],
            device_id=at(s, partner if k == 1 else lax.rem(p - PEER_OFFSETS[k] + nd, nd)),
            device_id_type=MESH,
        )

    def z_send(src_ref, slot, ch):
        z_copy(src_ref, slot, ch, 2).start()
        z_copy(src_ref, slot, ch, 0).start()

        @pl.when(jnp.logical_not(even))
        def _():
            z_copy(src_ref, slot, ch, 1).start()

    def relay(slot, ch):
        z_copy(own(slot, ch), slot, ch, 2).wait_recv()

        @pl.when(even)
        def _():
            z_copy(src.at[slot, rows(far + 1), cols(ch)], slot, ch, 1).start()

    def z_wait(slot, ch):
        for k in (0, 1):
            z_copy(own(slot, ch), slot, ch, k).wait_recv()

    def x_copy(c, ch):
        return pltpu.make_async_remote_copy(
            src_ref=stage.at[c, :, cols(ch)],
            dst_ref=src.at[0 if c == 0 else c + last, rows(0), cols(ch)],
            send_sem=xsend.at[c, ch],
            recv_sem=xrecv.at[c, ch],
            device_id=at(lax.rem(s + 1, ns), p),
            device_id_type=MESH,
        )

    def given(j, ch):
        return stacked.at[rows(j), cols(ch)]

    def own(slot, ch):
        return src.at[slot, rows(0), cols(ch)]

    tile = lax.broadcasted_iota(jnp.int32, (block, edges.shape[1]), 1) // block
    degree = []
    for c in range(slabs):
        entries = edges[rows(c), :].astype(jnp.float32)
        total = jnp.ones((block, 1), jnp.float32)
        for j in range(slabs):
            scale = jnp.full(entries.shape, 1.0 if c == j else 0.0, jnp.float32)
            for k in range(len(PEER_OFFSETS)):
                wanted = jnp.where(picks[c, k] == j, 1.0, 0.0)
                scale = jnp.where(tile == k + 1, wanted, scale)
            masked = entries * scale
            masks[c, j] = masked.astype(jnp.bfloat16)
            total = total + jnp.sum(masked, axis=1, keepdims=True)
        degree.append(total)
    for j in range(1, slabs):
        src[j, rows(0), :] = stacked[rows(j), :]

    @pl.when(s == 0)
    def _():
        src[0, rows(0), :] = stacked[rows(0), :]

    pl.semaphore_wait(barrier, len(greeted))

    for ch in range(nch):
        @pl.when(s == 0)
        def _():
            z_send(given(0, ch), 0, ch)
        for j in range(1, slabs):
            z_send(given(j, ch), j, ch)

    def gather(c, j, slot, ch):
        return jnp.dot(
            masks[c, j], src[slot, :, cols(ch)], preferred_element_type=jnp.float32
        )

    def self_part(slot):
        for ch in range(nch):
            part = jnp.dot(
                src[slot, rows(0), cols(ch)], ws[cols(ch), :],
                preferred_element_type=jnp.float32,
            )
            if ch == 0:
                acc[...] = part
            else:
                acc[...] += part

    def forward(c, ch):
        x_copy(c, ch).wait_recv()
        z_send(own(fresh_slot(c), ch), fresh_slot(c), ch)

    w_self.wait()

    @pl.when(s == 0)
    def _():
        self_part(0)

    for ch in range(nch):
        @pl.when(s == 0)
        def _():
            relay(0, ch)
        for j in range(1, slabs):
            relay(j, ch)

    w_neigh.wait()

    early = nch // 2
    for c in range(slabs):
        slot = fresh_slot(c)
        if c == 0:
            @pl.when(s > 0)
            def _():
                for ch in range(nch):
                    forward(0, ch)
                self_part(0)
        else:
            @pl.when(s > 1)
            def _():
                for ch in range(early, nch):
                    forward(c, ch)

            self_part(slot)
        for ch in range(nch):
            if c == 0:
                for j in range(1, slabs):
                    z_wait(j, ch)
            part = None
            for j in range(slabs):
                if j != c:
                    term = gather(c, j, fresh_slot(j) if j < c else j, ch)
                    part = term if part is None else part + term
            pre[:, cols(ch)] = part

        @pl.when(s > 0)
        def _():
            relay(slot, 0)
        for ch in range(nch):
            if ch == nch - 1 and c + 1 < slabs:
                @pl.when(s == 1)
                def _():
                    for n in range(nch):
                        forward(c + 1, n)

                @pl.when(s > 1)
                def _():
                    for n in range(early):
                        forward(c + 1, n)
            if c == 0:
                z_wait(slot, ch)

            @pl.when(s > 0)
            def _():
                if ch < nch - 1:
                    relay(slot, ch + 1)
                if c > 0:
                    z_wait(slot, ch)
            summed = pre[:, cols(ch)] + gather(c, c, slot, ch)
            mean = (summed / degree[c]).astype(jnp.bfloat16)
            if ch < nch - 1:
                acc[...] += jnp.dot(mean, wn[cols(ch), :], preferred_element_type=jnp.float32)
            else:
                for n in range(nch):
                    hidden = acc[:, cols(n)] + jnp.dot(
                        mean, wn[cols(ch), cols(n)], preferred_element_type=jnp.float32
                    )
                    stage[c, :, cols(n)] = jnp.maximum(hidden, 0.0).astype(jnp.bfloat16)

                    @pl.when(s < ns - 1)
                    def _():
                        x_copy(c, n).start()
        out[rows(c), :] = stage[c]

    for ch in range(nch):
        for k in range(len(PEER_OFFSETS)):
            for slot in range(slabs):
                z_copy(own(slot, ch), slot, ch, k).wait_send()
            for c in range(1, slabs):
                @pl.when(s > 0)
                def _():
                    z_copy(own(c + last, ch), c + last, ch, k).wait_send()
        for c in range(slabs):
            @pl.when(s < ns - 1)
            def _():
                x_copy(c, ch).wait_send()


def per_device(ns, nd, stacked, edges, picks, self_w, neigh_w):
    _, node_rows, width = stacked.shape
    tiles = len(PEER_OFFSETS) + 1
    block = edges.shape[1] // tiles
    slabs = node_rows // block
    nch = max(1, width // 256)
    slots = 2 * slabs - 1
    vmem = pl.BlockSpec(memory_space=pltpu.VMEM)
    hbm = pl.BlockSpec(memory_space=pl.ANY)
    result = pl.pallas_call(
        functools.partial(kernel, ns, nd, slabs, nch),
        out_shape=jax.ShapeDtypeStruct((node_rows, width), jnp.bfloat16),
        in_specs=[vmem, vmem, pl.BlockSpec(memory_space=pltpu.SMEM), hbm, hbm],
        out_specs=vmem,
        scratch_shapes=[
            pltpu.VMEM((width, width), jnp.bfloat16),
            pltpu.VMEM((width, width), jnp.bfloat16),
            pltpu.VMEM((slots, tiles * block, width), jnp.bfloat16),
            pltpu.VMEM((slabs, slabs, block, tiles * block), jnp.bfloat16),
            pltpu.VMEM((block, width), jnp.float32),
            pltpu.VMEM((block, width), jnp.float32),
            pltpu.VMEM((slabs, block, width), jnp.bfloat16),
            pltpu.SemaphoreType.DMA((2,)),
            pltpu.SemaphoreType.DMA((slots, nch, tiles - 1)),
            pltpu.SemaphoreType.DMA((slots, nch, tiles - 1)),
            pltpu.SemaphoreType.DMA((slabs, nch)),
            pltpu.SemaphoreType.DMA((slabs, nch)),
        ],
        compiler_params=pltpu.CompilerParams(collective_id=0, has_side_effects=True),
    )(stacked[0], edges, picks, self_w[0], neigh_w[0])
    return result[None]


def solution(mesh):
    in_specs = (
        P("section", "dom", None),
        P("dom", None),
        P("dom", None),
        P("section", None, None),
        P("section", None, None),
    )
    out_specs = P("section", "dom", None)
    ns, nd = mesh.shape["section"], mesh.shape["dom"]
    return jax.shard_map(
        functools.partial(per_device, ns, nd),
        mesh=mesh, in_specs=in_specs, out_specs=out_specs, check_vma=False,
    )
```

```python
import functools

import jax
import jax.numpy as jnp
from jax import lax
from jax.experimental import pallas as pl
from jax.experimental.pallas import tpu as pltpu
from jax.sharding import PartitionSpec as P

PEER_OFFSETS = (-1, 1, 2)
MESH = pl.DeviceIdType.MESH


def kernel(
    ns, nd, slabs, nch,
    stacked, edges, picks, ws_hbm, wn_hbm, out,
    ws, wn, src, masks, pre, acc, stage, above, sums, summed_below,
    wsem, zsend, zrecv, xsend, xrecv, psend, precv,
):
    block = edges.shape[1] // (len(PEER_OFFSETS) + 1)
    width = stacked.shape[1]
    cw = width // nch
    s = lax.axis_index("section")
    p = lax.axis_index("dom")

    def at(section, dom):
        return {"section": section, "dom": dom}

    w_self = pltpu.make_async_copy(ws_hbm, ws, wsem.at[0])
    w_neigh = pltpu.make_async_copy(wn_hbm, wn, wsem.at[1])
    w_self.start()
    w_neigh.start()

    barrier = pltpu.get_barrier_semaphore()
    greeted = [at(s, lax.rem(p + o + nd, nd)) for o in (-2, -1, 1, 2)]
    greeted += [at(lax.rem(s + 1, ns), p), at(lax.rem(s + ns - 1, ns), p)]
    for device in greeted:
        pl.semaphore_signal(barrier, inc=1, device_id=device, device_id_type=MESH)

    def rows(c):
        return pl.ds(c * block, block)

    def cols(ch):
        return pl.ds(ch * cw, cw)

    last = slabs - 1

    even = lax.rem(p, 2) == 0
    partner = p + 1 - 2 * lax.rem(p, 2)
    far = len(PEER_OFFSETS) - 1

    def z_copy(src_ref, slot, ch, k):
        return pltpu.make_async_remote_copy(
            src_ref=src_ref,
            dst_ref=src.at[slot, rows(k + 1), cols(ch)],
            send_sem=zsend.at[slot, ch, k],
            recv_sem=zrecv.at[slot, ch, k],
            device_id=at(s, partner if k == 1 and ch < nch - 1 else lax.rem(p - PEER_OFFSETS[k] + nd, nd)),
            device_id_type=MESH,
        )

    def z_send(src_ref, slot, ch):
        z_copy(src_ref, slot, ch, 2).start()
        z_copy(src_ref, slot, ch, 0).start()

        if ch == nch - 1:
            z_copy(src_ref, slot, ch, 1).start()
        else:
            @pl.when(jnp.logical_not(even))
            def _():
                z_copy(src_ref, slot, ch, 1).start()

    def relay(slot, ch):
        z_copy(own(slot, ch), slot, ch, 2).wait_recv()

        if ch < nch - 1:
            @pl.when(even)
            def _():
                z_copy(src.at[slot, rows(far + 1), cols(ch)], slot, ch, 1).start()

    def z_wait(slot, ch):
        for k in (0, 1):
            z_copy(own(slot, ch), slot, ch, k).wait_recv()

    def x_copy(c, ch):
        return pltpu.make_async_remote_copy(
            src_ref=stage.at[c, :, cols(ch)],
            dst_ref=src.at[0, rows(0), cols(ch)] if c == 0 else above.at[c - 1, :, cols(ch)],
            send_sem=xsend.at[c, ch],
            recv_sem=xrecv.at[c, ch],
            device_id=at(lax.rem(s + 1, ns), p),
            device_id_type=MESH,
        )

    def sum_copy(c, ch):
        return pltpu.make_async_remote_copy(
            src_ref=sums.at[c - 1, :, cols(ch)],
            dst_ref=summed_below.at[c - 1, :, cols(ch)],
            send_sem=psend.at[c - 1, ch],
            recv_sem=precv.at[c - 1, ch],
            device_id=at(lax.rem(s + 1, ns), p),
            device_id_type=MESH,
        )

    def given(j, ch):
        return stacked.at[rows(j), cols(ch)]

    def own(slot, ch):
        return src.at[slot, rows(0), cols(ch)]

    tile = lax.broadcasted_iota(jnp.int32, (block, edges.shape[1]), 1) // block
    degree = []
    for c in range(slabs):
        entries = edges[rows(c), :].astype(jnp.float32)
        total = jnp.ones((block, 1), jnp.float32)
        for j in range(slabs):
            scale = jnp.full(entries.shape, 1.0 if c == j else 0.0, jnp.float32)
            for k in range(len(PEER_OFFSETS)):
                wanted = jnp.where(picks[c, k] == j, 1.0, 0.0)
                scale = jnp.where(tile == k + 1, wanted, scale)
            masked = entries * scale
            masks[c, j] = masked.astype(jnp.bfloat16)
            total = total + jnp.sum(masked, axis=1, keepdims=True)
        degree.append(total)
    for j in range(1, slabs):
        src[j, rows(0), :] = stacked[rows(j), :]

    @pl.when(s == 0)
    def _():
        src[0, rows(0), :] = stacked[rows(0), :]

    pl.semaphore_wait(barrier, len(greeted))

    for ch in range(nch):
        @pl.when(s == 0)
        def _():
            z_send(given(0, ch), 0, ch)
        for j in range(1, slabs):
            z_send(given(j, ch), j, ch)

    def gather(c, j, slot, ch):
        return jnp.dot(
            masks[c, j], src[slot, :, cols(ch)], preferred_element_type=jnp.float32
        )

    def self_part(ref):
        for ch in range(nch):
            part = jnp.dot(
                ref[:, cols(ch)], ws[cols(ch), :], preferred_element_type=jnp.float32
            )
            if ch == 0:
                acc[...] = part
            else:
                acc[...] += part

    w_self.wait()

    @pl.when(s == 0)
    def _():
        self_part(src.at[0, rows(0)])

    for ch in range(nch):
        @pl.when(s == 0)
        def _():
            relay(0, ch)
        for j in range(1, slabs):
            relay(j, ch)

    w_neigh.wait()

    def produce(c, n, mean):
        hidden = acc[:, cols(n)] + jnp.dot(
            mean, wn[cols(nch - 1), cols(n)], preferred_element_type=jnp.float32
        )
        made = jnp.maximum(hidden, 0.0).astype(jnp.bfloat16)
        stage[c, :, cols(n)] = made
        out[rows(c), cols(n)] = made
        if c > 0:
            src[c + last, rows(0), cols(n)] = made

        @pl.when(s < ns - 1)
        def _():
            if c > 0:
                z_send(own(c + last, n), c + last, n)
            x_copy(c, n).start()

    def finish(c, ch, summed):
        mean = (summed / degree[c]).astype(jnp.bfloat16)
        if ch < nch - 1:
            acc[...] += jnp.dot(mean, wn[cols(ch), :], preferred_element_type=jnp.float32)
        else:
            for n in range(nch):
                produce(c, n, mean)

    @pl.when(s > 0)
    def _():
        for ch in range(nch):
            x_copy(0, ch).wait_recv()
            z_send(own(0, ch), 0, ch)
        self_part(src.at[0, rows(0)])

    for ch in range(nch):
        part = None
        for j in range(1, slabs):
            z_wait(j, ch)
            term = gather(0, j, j, ch)
            part = term if part is None else part + term
        pre[:, cols(ch)] = jnp.zeros((block, cw), jnp.float32) if part is None else part

    @pl.when(s > 0)
    def _():
        relay(0, 0)
    for ch in range(nch):
        z_wait(0, ch)
        if ch < nch - 1:
            @pl.when(s > 0)
            def _():
                relay(0, ch + 1)
        finish(0, ch, pre[:, cols(ch)] + gather(0, 0, 0, ch))

    for c in range(1, slabs):
        for ch in range(nch):
            part = gather(c, 0, 0, ch)
            for j in range(c + 1, slabs):
                part = part + gather(c, j, j, ch)
            pre[:, cols(ch)] = part

        @pl.when(s == 0)
        def _():
            self_part(src.at[c, rows(0)])
            for ch in range(nch):
                part = pre[:, cols(ch)]
                for j in range(1, c + 1):
                    part = part + gather(c, j, j, ch)
                pre[:, cols(ch)] = part

        @pl.when(s > 0)
        def _():
            for ch in range(nch):
                x_copy(c, ch).wait_recv()
            self_part(above.at[c - 1])

        for ch in range(nch):
            @pl.when(s > 0)
            def _():
                sum_copy(c, ch).wait_recv()
                pre[:, cols(ch)] += summed_below[c - 1, :, cols(ch)].astype(jnp.float32)
            finish(c, ch, pre[:, cols(ch)])

        @pl.when(s < ns - 1)
        def _():
            relay(c + last, 0)
            for ch in range(nch):
                if ch < nch - 1:
                    relay(c + last, ch + 1)
                z_wait(c + last, ch)
                part = None
                for j in range(1, c + 1):
                    term = gather(c, j, j + last, ch)
                    part = term if part is None else part + term
                sums[c - 1, :, cols(ch)] = part.astype(jnp.bfloat16)
                sum_copy(c, ch).start()

    for ch in range(nch):
        for k in range(len(PEER_OFFSETS)):
            for slot in range(slabs):
                z_copy(own(slot, ch), slot, ch, k).wait_send()

        @pl.when(s < ns - 1)
        def _():
            for c in range(slabs):
                x_copy(c, ch).wait_send()
            for c in range(1, slabs):
                sum_copy(c, ch).wait_send()
                for k in range(len(PEER_OFFSETS)):
                    z_copy(own(c + last, ch), c + last, ch, k).wait_send()


def per_device(ns, nd, stacked, edges, picks, self_w, neigh_w):
    _, node_rows, width = stacked.shape
    tiles = len(PEER_OFFSETS) + 1
    block = edges.shape[1] // tiles
    slabs = node_rows // block
    nch = max(1, width // 256)
    slots = 2 * slabs - 1
    others = max(1, slabs - 1)
    vmem = pl.BlockSpec(memory_space=pltpu.VMEM)
    hbm = pl.BlockSpec(memory_space=pl.ANY)
    result = pl.pallas_call(
        functools.partial(kernel, ns, nd, slabs, nch),
        out_shape=jax.ShapeDtypeStruct((node_rows, width), jnp.bfloat16),
        in_specs=[vmem, vmem, pl.BlockSpec(memory_space=pltpu.SMEM), hbm, hbm],
        out_specs=vmem,
        scratch_shapes=[
            pltpu.VMEM((width, width), jnp.bfloat16),
            pltpu.VMEM((width, width), jnp.bfloat16),
            pltpu.VMEM((slots, tiles * block, width), jnp.bfloat16),
            pltpu.VMEM((slabs, slabs, block, tiles * block), jnp.bfloat16),
            pltpu.VMEM((block, width), jnp.float32),
            pltpu.VMEM((block, width), jnp.float32),
            pltpu.VMEM((slabs, block, width), jnp.bfloat16),
            pltpu.VMEM((others, block, width), jnp.bfloat16),
            pltpu.VMEM((others, block, width), jnp.bfloat16),
            pltpu.VMEM((others, block, width), jnp.bfloat16),
            pltpu.SemaphoreType.DMA((2,)),
            pltpu.SemaphoreType.DMA((slots, nch, tiles - 1)),
            pltpu.SemaphoreType.DMA((slots, nch, tiles - 1)),
            pltpu.SemaphoreType.DMA((slabs, nch)),
            pltpu.SemaphoreType.DMA((slabs, nch)),
            pltpu.SemaphoreType.DMA((others, nch)),
            pltpu.SemaphoreType.DMA((others, nch)),
        ],
        compiler_params=pltpu.CompilerParams(collective_id=0, has_side_effects=True),
    )(stacked[0], edges, picks, self_w[0], neigh_w[0])
    return result[None]


def solution(mesh):
    in_specs = (
        P("section", "dom", None),
        P("dom", None),
        P("dom", None),
        P("section", None, None),
        P("section", None, None),
    )
    out_specs = P("section", "dom", None)
    ns, nd = mesh.shape["section"], mesh.shape["dom"]
    return jax.shard_map(
        functools.partial(per_device, ns, nd),
        mesh=mesh, in_specs=in_specs, out_specs=out_specs, check_vma=False,
    )
```

```python
import functools

import jax
import jax.numpy as jnp
from jax import lax
from jax.experimental import pallas as pl
from jax.experimental.pallas import tpu as pltpu
from jax.sharding import PartitionSpec as P

PEER_OFFSETS = (-1, 1, 2)
MESH = pl.DeviceIdType.MESH


def kernel(
    ns, nd, slabs, nch,
    stacked, edges, picks, ws_hbm, wn_hbm, out,
    ws, wn, src, masks, pre, acc, stage, above, sums, summed_below,
    wsem, zsend, zrecv, xsend, xrecv, psend, precv,
):
    block = edges.shape[1] // (len(PEER_OFFSETS) + 1)
    width = stacked.shape[1]
    cw = width // nch
    s = lax.axis_index("section")
    p = lax.axis_index("dom")

    def at(section, dom):
        return {"section": section, "dom": dom}

    w_self = pltpu.make_async_copy(ws_hbm, ws, wsem.at[0])
    w_neigh = pltpu.make_async_copy(wn_hbm, wn, wsem.at[1])
    w_self.start()
    w_neigh.start()

    barrier = pltpu.get_barrier_semaphore()
    greeted = [at(s, lax.rem(p + o + nd, nd)) for o in (-2, -1, 1, 2)]
    greeted += [at(lax.rem(s + 1, ns), p), at(lax.rem(s + ns - 1, ns), p)]
    for device in greeted:
        pl.semaphore_signal(barrier, inc=1, device_id=device, device_id_type=MESH)

    def rows(c):
        return pl.ds(c * block, block)

    def cols(ch):
        return pl.ds(ch * cw, cw)

    last = slabs - 1

    even = lax.rem(p, 2) == 0
    partner = p + 1 - 2 * lax.rem(p, 2)
    far = len(PEER_OFFSETS) - 1

    def z_copy(src_ref, slot, ch, k):
        return pltpu.make_async_remote_copy(
            src_ref=src_ref,
            dst_ref=src.at[slot, rows(k + 1), cols(ch)],
            send_sem=zsend.at[slot, ch, k],
            recv_sem=zrecv.at[slot, ch, k],
            device_id=at(s, partner if k == 1 else lax.rem(p - PEER_OFFSETS[k] + nd, nd)),
            device_id_type=MESH,
        )

    def z_send(src_ref, slot, ch):
        z_copy(src_ref, slot, ch, 0).start()
        z_copy(src_ref, slot, ch, 2).start()

        @pl.when(jnp.logical_not(even))
        def _():
            z_copy(src_ref, slot, ch, 1).start()

    def relay(slot, ch):
        z_copy(own(slot, ch), slot, ch, 2).wait_recv()

        @pl.when(even)
        def _():
            z_copy(src.at[slot, rows(far + 1), cols(ch)], slot, ch, 1).start()

    def z_wait(slot, ch):
        for k in (0, 1):
            z_copy(own(slot, ch), slot, ch, k).wait_recv()

    def x_copy(c, ch):
        return pltpu.make_async_remote_copy(
            src_ref=stage.at[c, :, cols(ch)],
            dst_ref=src.at[0, rows(0), cols(ch)] if c == 0 else above.at[c - 1, :, cols(ch)],
            send_sem=xsend.at[c, ch],
            recv_sem=xrecv.at[c, ch],
            device_id=at(lax.rem(s + 1, ns), p),
            device_id_type=MESH,
        )

    def sum_copy(c, ch):
        return pltpu.make_async_remote_copy(
            src_ref=sums.at[c - 1, :, cols(ch)],
            dst_ref=summed_below.at[c - 1, :, cols(ch)],
            send_sem=psend.at[c - 1, ch],
            recv_sem=precv.at[c - 1, ch],
            device_id=at(lax.rem(s + 1, ns), p),
            device_id_type=MESH,
        )

    def given(j, ch):
        return stacked.at[rows(j), cols(ch)]

    def own(slot, ch):
        return src.at[slot, rows(0), cols(ch)]

    tile = lax.broadcasted_iota(jnp.int32, (block, edges.shape[1]), 1) // block
    degree = []
    for c in range(slabs):
        entries = edges[rows(c), :].astype(jnp.float32)
        total = jnp.ones((block, 1), jnp.float32)
        for j in range(slabs):
            scale = jnp.full(entries.shape, 1.0 if c == j else 0.0, jnp.float32)
            for k in range(len(PEER_OFFSETS)):
                wanted = jnp.where(picks[c, k] == j, 1.0, 0.0)
                scale = jnp.where(tile == k + 1, wanted, scale)
            masked = entries * scale
            masks[c, j] = masked.astype(jnp.bfloat16)
            total = total + jnp.sum(masked, axis=1, keepdims=True)
        degree.append(total)
    for j in range(1, slabs):
        src[j, rows(0), :] = stacked[rows(j), :]

    @pl.when(s == 0)
    def _():
        src[0, rows(0), :] = stacked[rows(0), :]

    pl.semaphore_wait(barrier, len(greeted))

    for ch in range(nch):
        @pl.when(s == 0)
        def _():
            z_send(given(0, ch), 0, ch)
        for j in range(1, slabs):
            z_send(given(j, ch), j, ch)

    def gather(c, j, slot, ch):
        return jnp.dot(
            masks[c, j], src[slot, :, cols(ch)], preferred_element_type=jnp.float32
        )

    def self_part(ref):
        for ch in range(nch):
            part = jnp.dot(
                ref[:, cols(ch)], ws[cols(ch), :], preferred_element_type=jnp.float32
            )
            if ch == 0:
                acc[...] = part
            else:
                acc[...] += part

    w_self.wait()

    @pl.when(s == 0)
    def _():
        self_part(src.at[0, rows(0)])

    for ch in range(nch):
        @pl.when(s == 0)
        def _():
            relay(0, ch)
        for j in range(1, slabs):
            relay(j, ch)

    w_neigh.wait()

    def produce(c, n, mean):
        hidden = acc[:, cols(n)] + jnp.dot(
            mean, wn[cols(nch - 1), cols(n)], preferred_element_type=jnp.float32
        )
        made = jnp.maximum(hidden, 0.0).astype(jnp.bfloat16)
        stage[c, :, cols(n)] = made
        out[rows(c), cols(n)] = made
        if c > 0:
            src[c + last, rows(0), cols(n)] = made

        @pl.when(s < ns - 1)
        def _():
            if c > 0:
                z_send(own(c + last, n), c + last, n)
            x_copy(c, n).start()

    def finish(c, ch, summed):
        mean = (summed / degree[c]).astype(jnp.bfloat16)
        if ch < nch - 1:
            acc[...] += jnp.dot(mean, wn[cols(ch), :], preferred_element_type=jnp.float32)
        else:
            for n in range(nch):
                produce(c, n, mean)

    @pl.when(s > 0)
    def _():
        for ch in range(nch):
            x_copy(0, ch).wait_recv()
            z_send(own(0, ch), 0, ch)
        self_part(src.at[0, rows(0)])

    for ch in range(nch):
        part = None
        for j in range(1, slabs):
            z_wait(j, ch)
            term = gather(0, j, j, ch)
            part = term if part is None else part + term
        pre[:, cols(ch)] = jnp.zeros((block, cw), jnp.float32) if part is None else part

    @pl.when(s > 0)
    def _():
        relay(0, 0)
    for ch in range(nch):
        z_wait(0, ch)
        if ch < nch - 1:
            @pl.when(s > 0)
            def _():
                relay(0, ch + 1)
        finish(0, ch, pre[:, cols(ch)] + gather(0, 0, 0, ch))

    for c in range(1, slabs):
        for ch in range(nch):
            part = gather(c, 0, 0, ch)
            for j in range(c + 1, slabs):
                part = part + gather(c, j, j, ch)
            pre[:, cols(ch)] = part

        @pl.when(s == 0)
        def _():
            self_part(src.at[c, rows(0)])
            for ch in range(nch):
                part = pre[:, cols(ch)]
                for j in range(1, c + 1):
                    part = part + gather(c, j, j, ch)
                pre[:, cols(ch)] = part

        @pl.when(s > 0)
        def _():
            for ch in range(nch):
                x_copy(c, ch).wait_recv()
            self_part(above.at[c - 1])

        for ch in range(nch):
            @pl.when(s > 0)
            def _():
                sum_copy(c, ch).wait_recv()
                pre[:, cols(ch)] += summed_below[c - 1, :, cols(ch)].astype(jnp.float32)
            finish(c, ch, pre[:, cols(ch)])

        @pl.when(s < ns - 1)
        def _():
            relay(c + last, 0)
            for ch in range(nch):
                if ch < nch - 1:
                    relay(c + last, ch + 1)
                z_wait(c + last, ch)
                part = None
                for j in range(1, c + 1):
                    term = gather(c, j, j + last, ch)
                    part = term if part is None else part + term
                sums[c - 1, :, cols(ch)] = part.astype(jnp.bfloat16)
                sum_copy(c, ch).start()

    for ch in range(nch):
        for k in range(len(PEER_OFFSETS)):
            for slot in range(slabs):
                z_copy(own(slot, ch), slot, ch, k).wait_send()

        @pl.when(s < ns - 1)
        def _():
            for c in range(slabs):
                x_copy(c, ch).wait_send()
            for c in range(1, slabs):
                sum_copy(c, ch).wait_send()
                for k in range(len(PEER_OFFSETS)):
                    z_copy(own(c + last, ch), c + last, ch, k).wait_send()


def per_device(ns, nd, stacked, edges, picks, self_w, neigh_w):
    _, node_rows, width = stacked.shape
    tiles = len(PEER_OFFSETS) + 1
    block = edges.shape[1] // tiles
    slabs = node_rows // block
    nch = max(1, width // 256)
    slots = 2 * slabs - 1
    others = max(1, slabs - 1)
    vmem = pl.BlockSpec(memory_space=pltpu.VMEM)
    hbm = pl.BlockSpec(memory_space=pl.ANY)
    result = pl.pallas_call(
        functools.partial(kernel, ns, nd, slabs, nch),
        out_shape=jax.ShapeDtypeStruct((node_rows, width), jnp.bfloat16),
        in_specs=[vmem, vmem, pl.BlockSpec(memory_space=pltpu.SMEM), hbm, hbm],
        out_specs=vmem,
        scratch_shapes=[
            pltpu.VMEM((width, width), jnp.bfloat16),
            pltpu.VMEM((width, width), jnp.bfloat16),
            pltpu.VMEM((slots, tiles * block, width), jnp.bfloat16),
            pltpu.VMEM((slabs, slabs, block, tiles * block), jnp.bfloat16),
            pltpu.VMEM((block, width), jnp.float32),
            pltpu.VMEM((block, width), jnp.float32),
            pltpu.VMEM((slabs, block, width), jnp.bfloat16),
            pltpu.VMEM((others, block, width), jnp.bfloat16),
            pltpu.VMEM((others, block, width), jnp.bfloat16),
            pltpu.VMEM((others, block, width), jnp.bfloat16),
            pltpu.SemaphoreType.DMA((2,)),
            pltpu.SemaphoreType.DMA((slots, nch, tiles - 1)),
            pltpu.SemaphoreType.DMA((slots, nch, tiles - 1)),
            pltpu.SemaphoreType.DMA((slabs, nch)),
            pltpu.SemaphoreType.DMA((slabs, nch)),
            pltpu.SemaphoreType.DMA((others, nch)),
            pltpu.SemaphoreType.DMA((others, nch)),
        ],
        compiler_params=pltpu.CompilerParams(collective_id=0, has_side_effects=True),
    )(stacked[0], edges, picks, self_w[0], neigh_w[0])
    return result[None]


def solution(mesh):
    in_specs = (
        P("section", "dom", None),
        P("dom", None),
        P("dom", None),
        P("section", None, None),
        P("section", None, None),
    )
    out_specs = P("section", "dom", None)
    ns, nd = mesh.shape["section"], mesh.shape["dom"]
    return jax.shard_map(
        functools.partial(per_device, ns, nd),
        mesh=mesh, in_specs=in_specs, out_specs=out_specs, check_vma=False,
    )
```

```python
import functools

import jax
import jax.numpy as jnp
from jax import lax
from jax.experimental import pallas as pl
from jax.experimental.pallas import tpu as pltpu
from jax.sharding import PartitionSpec as P

PEER_OFFSETS = (-1, 1, 2)
MESH = pl.DeviceIdType.MESH


def kernel(
    ns, nd, slabs, nch,
    stacked, edges, picks, ws_hbm, wn_hbm, out,
    ws, wn, src, masks, pre, acc, stage, above, sums, summed_below,
    lent, lent_mean, aided_mean, mean_now,
    wsem, zsend, zrecv, xsend, xrecv, psend, precv,
    lsend, lrecv, msend, mrecv, lzsend, lzrecv,
):
    block = edges.shape[1] // (len(PEER_OFFSETS) + 1)
    width = stacked.shape[1]
    cw = width // nch
    s = lax.axis_index("section")
    p = lax.axis_index("dom")

    def at(section, dom):
        return {"section": section, "dom": dom}

    w_self = pltpu.make_async_copy(ws_hbm, ws, wsem.at[0])
    w_neigh = pltpu.make_async_copy(wn_hbm, wn, wsem.at[1])
    w_self.start()
    w_neigh.start()

    barrier = pltpu.get_barrier_semaphore()
    greeted = [at(s, lax.rem(p + o + nd, nd)) for o in (-2, -1, 1, 2)]
    greeted += [at(lax.rem(s + 1, ns), p), at(lax.rem(s + ns - 1, ns), p)]
    for device in greeted:
        pl.semaphore_signal(barrier, inc=1, device_id=device, device_id_type=MESH)

    def rows(c):
        return pl.ds(c * block, block)

    def cols(ch):
        return pl.ds(ch * cw, cw)

    last = slabs - 1

    even = lax.rem(p, 2) == 0
    partner = p + 1 - 2 * lax.rem(p, 2)
    far = len(PEER_OFFSETS) - 1

    def z_copy(src_ref, slot, ch, k):
        return pltpu.make_async_remote_copy(
            src_ref=src_ref,
            dst_ref=src.at[slot, rows(k + 1), cols(ch)],
            send_sem=zsend.at[slot, ch, k],
            recv_sem=zrecv.at[slot, ch, k],
            device_id=at(s, partner if k == 1 else lax.rem(p - PEER_OFFSETS[k] + nd, nd)),
            device_id_type=MESH,
        )

    def z_send(src_ref, slot, ch):
        z_copy(src_ref, slot, ch, 0).start()
        z_copy(src_ref, slot, ch, 2).start()

        @pl.when(jnp.logical_not(even))
        def _():
            z_copy(src_ref, slot, ch, 1).start()

    def relay(slot, ch):
        z_copy(own(slot, ch), slot, ch, 2).wait_recv()

        @pl.when(even)
        def _():
            z_copy(src.at[slot, rows(far + 1), cols(ch)], slot, ch, 1).start()

    def z_wait(slot, ch):
        for k in (0, 1):
            z_copy(own(slot, ch), slot, ch, k).wait_recv()

    def x_copy(c, ch):
        return pltpu.make_async_remote_copy(
            src_ref=stage.at[c, :, cols(ch)],
            dst_ref=src.at[0, rows(0), cols(ch)] if c == 0 else above.at[c - 1, :, cols(ch)],
            send_sem=xsend.at[c, ch],
            recv_sem=xrecv.at[c, ch],
            device_id=at(lax.rem(s + 1, ns), p),
            device_id_type=MESH,
        )

    def sum_copy(c, ch):
        return pltpu.make_async_remote_copy(
            src_ref=sums.at[c - 1, :, cols(ch)],
            dst_ref=summed_below.at[c - 1, :, cols(ch)],
            send_sem=psend.at[c - 1, ch],
            recv_sem=precv.at[c - 1, ch],
            device_id=at(lax.rem(s + 1, ns), p),
            device_id_type=MESH,
        )

    def own(slot, ch):
        return src.at[slot, rows(0), cols(ch)]

    tile = lax.broadcasted_iota(jnp.int32, (block, edges.shape[1]), 1) // block
    degree = []
    for c in range(slabs):
        entries = edges[rows(c), :].astype(jnp.float32)
        total = jnp.ones((block, 1), jnp.float32)
        for j in range(slabs):
            scale = jnp.full(entries.shape, 1.0 if c == j else 0.0, jnp.float32)
            for k in range(len(PEER_OFFSETS)):
                wanted = jnp.where(picks[c, k] == j, 1.0, 0.0)
                scale = jnp.where(tile == k + 1, wanted, scale)
            masked = entries * scale
            masks[c, j] = masked.astype(jnp.bfloat16)
            total = total + jnp.sum(masked, axis=1, keepdims=True)
        degree.append(total)
    for j in range(1, slabs):
        src[j, rows(0), :] = stacked[rows(j), :]

    @pl.when(s == 0)
    def _():
        src[0, rows(0), :] = stacked[rows(0), :]

    pl.semaphore_wait(barrier, len(greeted))

    aided = nch - 1

    def lend_copy(j):
        return pltpu.make_async_remote_copy(
            src_ref=own(j, aided),
            dst_ref=lent.at[j, rows(0)],
            send_sem=lsend.at[j],
            recv_sem=lrecv.at[j],
            device_id=at(lax.rem(s + 1, ns), p),
            device_id_type=MESH,
        )

    def lent_copy(src_row, j, k):
        return pltpu.make_async_remote_copy(
            src_ref=lent.at[j, rows(src_row)],
            dst_ref=lent.at[j, rows(k + 1)],
            send_sem=lzsend.at[j, k],
            recv_sem=lzrecv.at[j, k],
            device_id=at(s, partner if k == 1 else lax.rem(p - PEER_OFFSETS[k] + nd, nd)),
            device_id_type=MESH,
        )

    def mean_copy(c):
        return pltpu.make_async_remote_copy(
            src_ref=lent_mean.at[c],
            dst_ref=aided_mean.at[c],
            send_sem=msend.at[c],
            recv_sem=mrecv.at[c],
            device_id=at(lax.rem(s + ns - 1, ns), p),
            device_id_type=MESH,
        )

    @pl.when(s == 0)
    def _():
        for j in range(slabs):
            lend_copy(j).start()

    @pl.when(s == 1)
    def _():
        for j in range(slabs):
            lend_copy(j).wait_recv()
            lent_copy(0, j, 0).start()
            lent_copy(0, j, 2).start()

            @pl.when(jnp.logical_not(even))
            def _():
                lent_copy(0, j, 1).start()

    for ch in range(nch):
        if ch != aided:
            @pl.when(s == 0)
            def _():
                z_send(own(0, ch), 0, ch)
            for j in range(1, slabs):
                z_send(own(j, ch), j, ch)
        else:
            @pl.when(s > 0)
            def _():
                for j in range(1, slabs):
                    z_send(own(j, ch), j, ch)

    def gather(c, j, slot, ch):
        return jnp.dot(
            masks[c, j], src[slot, :, cols(ch)], preferred_element_type=jnp.float32
        )

    def self_part(ref):
        for ch in range(nch):
            part = jnp.dot(
                ref[:, cols(ch)], ws[cols(ch), :], preferred_element_type=jnp.float32
            )
            if ch == 0:
                acc[...] = part
            else:
                acc[...] += part

    w_self.wait()

    @pl.when(s == 0)
    def _():
        self_part(src.at[0, rows(0)])

    @pl.when(s == 1)
    def _():
        for j in range(slabs):
            lent_copy(0, j, 2).wait_recv()

            @pl.when(even)
            def _():
                lent_copy(far + 1, j, 1).start()
        for j in range(slabs):
            for k in (0, 1):
                lent_copy(0, j, k).wait_recv()
        for c in range(slabs):
            summed = None
            for j in range(slabs):
                term = jnp.dot(masks[c, j], lent[j], preferred_element_type=jnp.float32)
                summed = term if summed is None else summed + term
            lent_mean[c] = (summed / degree[c]).astype(jnp.bfloat16)
            mean_copy(c).start()

    for ch in range(nch):
        if ch != aided:
            @pl.when(s == 0)
            def _():
                relay(0, ch)
            for j in range(1, slabs):
                relay(j, ch)
        else:
            @pl.when(s > 0)
            def _():
                for j in range(1, slabs):
                    relay(j, ch)

    w_neigh.wait()

    def produce(c, n, mean):
        hidden = acc[:, cols(n)] + jnp.dot(
            mean, wn[cols(nch - 1), cols(n)], preferred_element_type=jnp.float32
        )
        made = jnp.maximum(hidden, 0.0).astype(jnp.bfloat16)
        stage[c, :, cols(n)] = made
        out[rows(c), cols(n)] = made
        if c > 0:
            src[c + last, rows(0), cols(n)] = made

        @pl.when(s < ns - 1)
        def _():
            if c > 0:
                z_send(own(c + last, n), c + last, n)
            x_copy(c, n).start()

    def finish(c, ch, mean):
        if ch < nch - 1:
            acc[...] += jnp.dot(mean, wn[cols(ch), :], preferred_element_type=jnp.float32)
        else:
            for n in range(nch):
                produce(c, n, mean)

    def mean_of(c, summed):
        return (summed / degree[c]).astype(jnp.bfloat16)

    def use_aid(c):
        @pl.when(s == 0)
        def _():
            mean_copy(c).wait_recv()
            mean_now[...] = aided_mean[c]

    @pl.when(s > 0)
    def _():
        for ch in range(nch):
            x_copy(0, ch).wait_recv()
            z_send(own(0, ch), 0, ch)
        self_part(src.at[0, rows(0)])

    def history(ch):
        part = jnp.zeros((block, cw), jnp.float32)
        for j in range(1, slabs):
            z_wait(j, ch)
            part = part + gather(0, j, j, ch)
        pre[:, cols(ch)] = part

    for ch in range(nch):
        if ch != aided:
            history(ch)
        else:
            pl.when(s > 0)(functools.partial(history, ch))

    @pl.when(s > 0)
    def _():
        relay(0, 0)
    for ch in range(nch):
        if ch == aided:
            @pl.when(s > 0)
            def _():
                z_wait(0, ch)
                mean_now[...] = mean_of(0, pre[:, cols(ch)] + gather(0, 0, 0, ch))
            use_aid(0)
            finish(0, ch, mean_now[...])
        else:
            z_wait(0, ch)

            @pl.when(s > 0)
            def _():
                relay(0, ch + 1)
            finish(0, ch, mean_of(0, pre[:, cols(ch)] + gather(0, 0, 0, ch)))

    for c in range(1, slabs):
        def present(ch):
            part = gather(c, 0, 0, ch)
            for j in range(c + 1, slabs):
                part = part + gather(c, j, j, ch)
            pre[:, cols(ch)] = part

        for ch in range(nch):
            if ch != aided:
                present(ch)
            else:
                pl.when(s > 0)(functools.partial(present, ch))

        @pl.when(s == 0)
        def _():
            self_part(src.at[c, rows(0)])
            for ch in range(aided):
                part = pre[:, cols(ch)]
                for j in range(1, c + 1):
                    part = part + gather(c, j, j, ch)
                pre[:, cols(ch)] = part

        @pl.when(s > 0)
        def _():
            for ch in range(nch):
                x_copy(c, ch).wait_recv()
            self_part(above.at[c - 1])

        for ch in range(nch):
            @pl.when(s > 0)
            def _():
                sum_copy(c, ch).wait_recv()
                pre[:, cols(ch)] += summed_below[c - 1, :, cols(ch)].astype(jnp.float32)
            if ch == aided:
                @pl.when(s > 0)
                def _():
                    mean_now[...] = mean_of(c, pre[:, cols(ch)])
                use_aid(c)
                finish(c, ch, mean_now[...])
            else:
                finish(c, ch, mean_of(c, pre[:, cols(ch)]))

        @pl.when(s < ns - 1)
        def _():
            relay(c + last, 0)
            for ch in range(nch):
                if ch < nch - 1:
                    relay(c + last, ch + 1)
                z_wait(c + last, ch)
                part = None
                for j in range(1, c + 1):
                    term = gather(c, j, j + last, ch)
                    part = term if part is None else part + term
                sums[c - 1, :, cols(ch)] = part.astype(jnp.bfloat16)
                sum_copy(c, ch).start()

    for ch in range(nch):
        for k in range(len(PEER_OFFSETS)):
            for slot in range(slabs):
                if ch == aided:
                    pl.when(s > 0)(z_copy(own(slot, ch), slot, ch, k).wait_send)
                else:
                    z_copy(own(slot, ch), slot, ch, k).wait_send()

        @pl.when(s < ns - 1)
        def _():
            for c in range(slabs):
                x_copy(c, ch).wait_send()
            for c in range(1, slabs):
                sum_copy(c, ch).wait_send()
                for k in range(len(PEER_OFFSETS)):
                    z_copy(own(c + last, ch), c + last, ch, k).wait_send()


    @pl.when(s == 0)
    def _():
        for j in range(slabs):
            lend_copy(j).wait_send()

    @pl.when(s == 1)
    def _():
        for j in range(slabs):
            for k in range(len(PEER_OFFSETS)):
                lent_copy(0, j, k).wait_send()
            mean_copy(j).wait_send()


def per_device(ns, nd, stacked, edges, picks, self_w, neigh_w):
    _, node_rows, width = stacked.shape
    tiles = len(PEER_OFFSETS) + 1
    block = edges.shape[1] // tiles
    slabs = node_rows // block
    nch = max(1, width // 256)
    slots = 2 * slabs - 1
    others = max(1, slabs - 1)
    vmem = pl.BlockSpec(memory_space=pltpu.VMEM)
    hbm = pl.BlockSpec(memory_space=pl.ANY)
    result = pl.pallas_call(
        functools.partial(kernel, ns, nd, slabs, nch),
        out_shape=jax.ShapeDtypeStruct((node_rows, width), jnp.bfloat16),
        in_specs=[vmem, vmem, pl.BlockSpec(memory_space=pltpu.SMEM), hbm, hbm],
        out_specs=vmem,
        scratch_shapes=[
            pltpu.VMEM((width, width), jnp.bfloat16),
            pltpu.VMEM((width, width), jnp.bfloat16),
            pltpu.VMEM((slots, tiles * block, width), jnp.bfloat16),
            pltpu.VMEM((slabs, slabs, block, tiles * block), jnp.bfloat16),
            pltpu.VMEM((block, width), jnp.float32),
            pltpu.VMEM((block, width), jnp.float32),
            pltpu.VMEM((slabs, block, width), jnp.bfloat16),
            pltpu.VMEM((others, block, width), jnp.bfloat16),
            pltpu.VMEM((others, block, width), jnp.bfloat16),
            pltpu.VMEM((others, block, width), jnp.bfloat16),
            pltpu.VMEM((slabs, tiles * block, width // nch), jnp.bfloat16),
            pltpu.VMEM((slabs, block, width // nch), jnp.bfloat16),
            pltpu.VMEM((slabs, block, width // nch), jnp.bfloat16),
            pltpu.VMEM((block, width // nch), jnp.bfloat16),
            pltpu.SemaphoreType.DMA((2,)),
            pltpu.SemaphoreType.DMA((slots, nch, tiles - 1)),
            pltpu.SemaphoreType.DMA((slots, nch, tiles - 1)),
            pltpu.SemaphoreType.DMA((slabs, nch)),
            pltpu.SemaphoreType.DMA((slabs, nch)),
            pltpu.SemaphoreType.DMA((others, nch)),
            pltpu.SemaphoreType.DMA((others, nch)),
            pltpu.SemaphoreType.DMA((slabs,)),
            pltpu.SemaphoreType.DMA((slabs,)),
            pltpu.SemaphoreType.DMA((slabs,)),
            pltpu.SemaphoreType.DMA((slabs,)),
            pltpu.SemaphoreType.DMA((slabs, tiles - 1)),
            pltpu.SemaphoreType.DMA((slabs, tiles - 1)),
        ],
        compiler_params=pltpu.CompilerParams(collective_id=0, has_side_effects=True),
    )(stacked[0], edges, picks, self_w[0], neigh_w[0])
    return result[None]


def solution(mesh):
    in_specs = (
        P("section", "dom", None),
        P("dom", None),
        P("dom", None),
        P("section", None, None),
        P("section", None, None),
    )
    out_specs = P("section", "dom", None)
    ns, nd = mesh.shape["section"], mesh.shape["dom"]
    return jax.shard_map(
        functools.partial(per_device, ns, nd),
        mesh=mesh, in_specs=in_specs, out_specs=out_specs, check_vma=False,
    )
```

```python
import functools

import jax
import jax.numpy as jnp
from jax import lax
from jax.experimental import pallas as pl
from jax.experimental.pallas import tpu as pltpu
from jax.sharding import PartitionSpec as P

PEER_OFFSETS = (-1, 1, 2)
MESH = pl.DeviceIdType.MESH


def kernel(
    ns, nd, slabs, nch,
    stacked, edges, picks, ws_hbm, wn_hbm, out,
    ws, wn, src, masks, pre, acc, stage, above, sums, summed_below,
    wsem, zsend, zrecv, xsend, xrecv, psend, precv,
):
    block = edges.shape[1] // (len(PEER_OFFSETS) + 1)
    width = stacked.shape[1]
    cw = width // nch
    s = lax.axis_index("section")
    p = lax.axis_index("dom")

    def at(section, dom):
        return {"section": section, "dom": dom}

    w_self = pltpu.make_async_copy(ws_hbm, ws, wsem.at[0])
    w_neigh = pltpu.make_async_copy(wn_hbm, wn, wsem.at[1])
    w_self.start()
    w_neigh.start()

    barrier = pltpu.get_barrier_semaphore()
    greeted = [at(s, lax.rem(p + o + nd, nd)) for o in (-2, -1, 1, 2)]
    greeted += [at(lax.rem(s + 1, ns), p), at(lax.rem(s + ns - 1, ns), p)]
    for device in greeted:
        pl.semaphore_signal(barrier, inc=1, device_id=device, device_id_type=MESH)

    def rows(c):
        return pl.ds(c * block, block)

    def cols(ch):
        return pl.ds(ch * cw, cw)

    last = slabs - 1

    even = lax.rem(p, 2) == 0
    partner = p + 1 - 2 * lax.rem(p, 2)
    far = len(PEER_OFFSETS) - 1

    def z_copy(src_ref, slot, ch, k):
        return pltpu.make_async_remote_copy(
            src_ref=src_ref,
            dst_ref=src.at[slot, rows(k + 1), cols(ch)],
            send_sem=zsend.at[slot, ch, k],
            recv_sem=zrecv.at[slot, ch, k],
            device_id=at(s, partner if k == 1 else lax.rem(p - PEER_OFFSETS[k] + nd, nd)),
            device_id_type=MESH,
        )

    def z_send(src_ref, slot, ch):
        z_copy(src_ref, slot, ch, 0).start()
        z_copy(src_ref, slot, ch, 2).start()

        @pl.when(jnp.logical_not(even))
        def _():
            z_copy(src_ref, slot, ch, 1).start()

    def relay(slot, ch):
        z_copy(own(slot, ch), slot, ch, 2).wait_recv()

        @pl.when(even)
        def _():
            z_copy(src.at[slot, rows(far + 1), cols(ch)], slot, ch, 1).start()

    def z_wait(slot, ch):
        for k in (0, 1):
            z_copy(own(slot, ch), slot, ch, k).wait_recv()

    def x_copy(c, ch):
        return pltpu.make_async_remote_copy(
            src_ref=stage.at[c, :, cols(ch)],
            dst_ref=src.at[0, rows(0), cols(ch)] if c == 0 else above.at[c - 1, :, cols(ch)],
            send_sem=xsend.at[c, ch],
            recv_sem=xrecv.at[c, ch],
            device_id=at(lax.rem(s + 1, ns), p),
            device_id_type=MESH,
        )

    def sum_copy(c, ch):
        return pltpu.make_async_remote_copy(
            src_ref=sums.at[c - 1, :, cols(ch)],
            dst_ref=summed_below.at[c - 1, :, cols(ch)],
            send_sem=psend.at[c - 1, ch],
            recv_sem=precv.at[c - 1, ch],
            device_id=at(lax.rem(s + 1, ns), p),
            device_id_type=MESH,
        )

    def given(j, ch):
        return stacked.at[rows(j), cols(ch)]

    def own(slot, ch):
        return src.at[slot, rows(0), cols(ch)]

    tile = lax.broadcasted_iota(jnp.int32, (block, edges.shape[1]), 1) // block
    degree = []
    for c in range(slabs):
        entries = edges[rows(c), :].astype(jnp.float32)
        total = jnp.ones((block, 1), jnp.float32)
        for j in range(slabs):
            scale = jnp.full(entries.shape, 1.0 if c == j else 0.0, jnp.float32)
            for k in range(len(PEER_OFFSETS)):
                wanted = jnp.where(picks[c, k] == j, 1.0, 0.0)
                scale = jnp.where(tile == k + 1, wanted, scale)
            masked = entries * scale
            masks[c, j] = masked.astype(jnp.bfloat16)
            total = total + jnp.sum(masked, axis=1, keepdims=True)
        degree.append(total)
    for j in range(1, slabs):
        src[j, rows(0), :] = stacked[rows(j), :]

    @pl.when(s == 0)
    def _():
        src[0, rows(0), :] = stacked[rows(0), :]

    pl.semaphore_wait(barrier, len(greeted))

    for ch in range(nch):
        @pl.when(s == 0)
        def _():
            z_send(given(0, ch), 0, ch)
        for j in range(1, slabs):
            z_send(given(j, ch), j, ch)

    def gather(c, j, slot, ch):
        return jnp.dot(
            masks[c, j], src[slot, :, cols(ch)], preferred_element_type=jnp.float32
        )

    def self_part(ref):
        for ch in range(nch):
            part = jnp.dot(
                ref[:, cols(ch)], ws[cols(ch), :], preferred_element_type=jnp.float32
            )
            if ch == 0:
                acc[...] = part
            else:
                acc[...] += part

    w_self.wait()

    @pl.when(s == 0)
    def _():
        self_part(src.at[0, rows(0)])

    for ch in range(nch):
        @pl.when(s == 0)
        def _():
            relay(0, ch)
        for j in range(1, slabs):
            relay(j, ch)

    w_neigh.wait()

    def produce(c, n, mean):
        hidden = acc[:, cols(n)] + jnp.dot(
            mean, wn[cols(nch - 1), cols(n)], preferred_element_type=jnp.float32
        )
        made = jnp.maximum(hidden, 0.0).astype(jnp.bfloat16)
        stage[c, :, cols(n)] = made
        out[rows(c), cols(n)] = made
        if c > 0:
            src[c + last, rows(0), cols(n)] = made

        @pl.when(s < ns - 1)
        def _():
            if c > 0:
                z_send(own(c + last, n), c + last, n)
            x_copy(c, n).start()

    def finish(c, ch, summed):
        mean = (summed / degree[c]).astype(jnp.bfloat16)
        if ch < nch - 1:
            acc[...] += jnp.dot(mean, wn[cols(ch), :], preferred_element_type=jnp.float32)
        else:
            for n in range(nch):
                produce(c, n, mean)

    @pl.when(s > 0)
    def _():
        for ch in range(nch):
            x_copy(0, ch).wait_recv()
            z_send(own(0, ch), 0, ch)
        self_part(src.at[0, rows(0)])

    for ch in range(nch):
        part = None
        for j in range(1, slabs):
            z_wait(j, ch)
            term = gather(0, j, j, ch)
            part = term if part is None else part + term
        pre[:, cols(ch)] = jnp.zeros((block, cw), jnp.float32) if part is None else part

    @pl.when(s > 0)
    def _():
        for ch in range(nch):
            relay(0, ch)
    for ch in range(nch):
        z_wait(0, ch)
        finish(0, ch, pre[:, cols(ch)] + gather(0, 0, 0, ch))

    for c in range(1, slabs):
        for ch in range(nch):
            part = gather(c, 0, 0, ch)
            for j in range(c + 1, slabs):
                part = part + gather(c, j, j, ch)
            pre[:, cols(ch)] = part

        @pl.when(s == 0)
        def _():
            self_part(src.at[c, rows(0)])
            for ch in range(nch):
                part = pre[:, cols(ch)]
                for j in range(1, c + 1):
                    part = part + gather(c, j, j, ch)
                pre[:, cols(ch)] = part

        @pl.when(s > 0)
        def _():
            for ch in range(nch):
                x_copy(c, ch).wait_recv()
            self_part(above.at[c - 1])

        for ch in range(nch):
            @pl.when(s > 0)
            def _():
                sum_copy(c, ch).wait_recv()
                pre[:, cols(ch)] += summed_below[c - 1, :, cols(ch)].astype(jnp.float32)
            finish(c, ch, pre[:, cols(ch)])

        @pl.when(s < ns - 1)
        def _():
            for ch in range(nch):
                relay(c + last, ch)
            for ch in range(nch):
                z_wait(c + last, ch)
                part = None
                for j in range(1, c + 1):
                    term = gather(c, j, j + last, ch)
                    part = term if part is None else part + term
                sums[c - 1, :, cols(ch)] = part.astype(jnp.bfloat16)
                sum_copy(c, ch).start()

    for ch in range(nch):
        for k in range(len(PEER_OFFSETS)):
            for slot in range(slabs):
                z_copy(own(slot, ch), slot, ch, k).wait_send()

        @pl.when(s < ns - 1)
        def _():
            for c in range(slabs):
                x_copy(c, ch).wait_send()
            for c in range(1, slabs):
                sum_copy(c, ch).wait_send()
                for k in range(len(PEER_OFFSETS)):
                    z_copy(own(c + last, ch), c + last, ch, k).wait_send()


def per_device(ns, nd, stacked, edges, picks, self_w, neigh_w):
    _, node_rows, width = stacked.shape
    tiles = len(PEER_OFFSETS) + 1
    block = edges.shape[1] // tiles
    slabs = node_rows // block
    nch = max(1, width // 256)
    slots = 2 * slabs - 1
    others = max(1, slabs - 1)
    vmem = pl.BlockSpec(memory_space=pltpu.VMEM)
    hbm = pl.BlockSpec(memory_space=pl.ANY)
    result = pl.pallas_call(
        functools.partial(kernel, ns, nd, slabs, nch),
        out_shape=jax.ShapeDtypeStruct((node_rows, width), jnp.bfloat16),
        in_specs=[vmem, vmem, pl.BlockSpec(memory_space=pltpu.SMEM), hbm, hbm],
        out_specs=vmem,
        scratch_shapes=[
            pltpu.VMEM((width, width), jnp.bfloat16),
            pltpu.VMEM((width, width), jnp.bfloat16),
            pltpu.VMEM((slots, tiles * block, width), jnp.bfloat16),
            pltpu.VMEM((slabs, slabs, block, tiles * block), jnp.bfloat16),
            pltpu.VMEM((block, width), jnp.float32),
            pltpu.VMEM((block, width), jnp.float32),
            pltpu.VMEM((slabs, block, width), jnp.bfloat16),
            pltpu.VMEM((others, block, width), jnp.bfloat16),
            pltpu.VMEM((others, block, width), jnp.bfloat16),
            pltpu.VMEM((others, block, width), jnp.bfloat16),
            pltpu.SemaphoreType.DMA((2,)),
            pltpu.SemaphoreType.DMA((slots, nch, tiles - 1)),
            pltpu.SemaphoreType.DMA((slots, nch, tiles - 1)),
            pltpu.SemaphoreType.DMA((slabs, nch)),
            pltpu.SemaphoreType.DMA((slabs, nch)),
            pltpu.SemaphoreType.DMA((others, nch)),
            pltpu.SemaphoreType.DMA((others, nch)),
        ],
        compiler_params=pltpu.CompilerParams(collective_id=0, has_side_effects=True),
    )(stacked[0], edges, picks, self_w[0], neigh_w[0])
    return result[None]


def solution(mesh):
    in_specs = (
        P("section", "dom", None),
        P("dom", None),
        P("dom", None),
        P("section", None, None),
        P("section", None, None),
    )
    out_specs = P("section", "dom", None)
    ns, nd = mesh.shape["section"], mesh.shape["dom"]
    return jax.shard_map(
        functools.partial(per_device, ns, nd),
        mesh=mesh, in_specs=in_specs, out_specs=out_specs, check_vma=False,
    )
```
